128 devices in a mesh: gx: 16 (over x_hi, y, core), gy: 8 (over x_lo, z).
Axes of the slice: x: 4 (x_hi: 2, x_lo: 2; x = x_hi * 2 + x_lo), y: 4, z: 4, core: 2. Of those that a mesh axis runs over, the one named last changes fastest.
Arguments:
- values: bfloat16 [128, 32, 6, 128, 128], P('gx', 'gy'), may hold values from 0.019897461 to 1
- columns: int32 [128, 32, 6], P('gx', 'gy'), may hold values from 0 to 4095, as said below
- panel: float32 [128, 32, 128, 128], P('gx', 'gy'), as said below
Outputs:
- first_embedding: float32 [128, 32, 128, 128], P('gx', 'gy')
- embedding: float32 [128, 32, 128, 128], P('gx', 'gy')
- ritz: float32 [128, 128], replicated
The draws below stay inside these ranges and needn't reach their ends.
Inputs may be any that keep to these rules, and one draw needn't show every extreme that they name: Each block column lies within one block of its block row along both grid directions: |columns // 32 - p| <= 1 and |columns % 32 - q| <= 1. `panel`: finite entries.
All inputs are finite; a program needn't handle non-finite values.
Results may differ from the reference program's by a relative error of at most 0.0003.
The reference program's roundings to bfloat16 on the way count: a program that leaves them out, or rounds other values in their place, can miss the bound.
Values may be sent and summed in bfloat16 or wider, within the bound.
A program may use at most 64 MiB of HBM per device.

```python
import math
import jax
import jax.numpy as jnp
from jax import lax

BLOCK = 128
PANEL = 128
K = 6
NBX = 128
NBY = 32
ROWS = 524288


def draw_columns(key, part):
    key_score = jax.random.fold_in(key, 11)
    scores = jax.random.randint(key_score, (NBX, NBY, 9), 0, 1000) * 16 + jnp.arange(9, dtype=jnp.int32)
    order = jnp.argsort(scores, axis=-1, stable=True)[..., :K].astype(jnp.int32)
    off_x = order // 3 - 1
    off_y = order % 3 - 1
    row_x = jnp.arange(NBX, dtype=jnp.int32)[:, None, None]
    row_y = jnp.arange(NBY, dtype=jnp.int32)[None, :, None]
    target_x = row_x + off_x
    target_x = jnp.where(target_x < 0, row_x - off_x, target_x)
    target_x = jnp.where(target_x >= NBX, row_x - off_x, target_x)
    target_y = row_y + off_y
    target_y = jnp.where(target_y < 0, row_y - off_y, target_y)
    target_y = jnp.where(target_y >= NBY, row_y - off_y, target_y)
    return (target_x * NBY + target_y).astype(jnp.int32)


def draw_panel(key, part):
    key_entry = jax.random.fold_in(key, 23)
    shape = (NBX, NBY, BLOCK, PANEL)
    position = (jnp.arange(NBX, dtype=jnp.float32)[:, None] * NBY + jnp.arange(NBY, dtype=jnp.float32)[None, :]) / (NBX * NBY - 1)
    entries = jax.random.truncated_normal(key_entry, -6.0, 6.0, shape, jnp.float32)
    rise = jnp.exp(jnp.log(6.0) * position)
    return (entries * rise[:, :, None, None]).astype(jnp.float32)


def level_of(stream_key, dims, cuts, low, high):
    level = 1.0
    for axis_at, shards_of in cuts:
        draws = jax.random.uniform(jax.random.fold_in(jax.random.fold_in(stream_key, 6), axis_at), (shards_of,), jnp.float32, low / len(cuts), high / len(cuts))
        level = level * jnp.repeat(jnp.exp(draws), dims[axis_at] // shards_of).reshape((-1,) + (1,) * (len(dims) - 1 - axis_at))
    return level


def setup_inputs(seed: int = 0) -> dict:
    key_of = jax.random.split(jax.random.key(seed), 4)
    return {
        "values": jnp.clip(jnp.exp(math.log(1.0) - 3.9171631 * jax.random.uniform(key_of[0], (NBX, NBY, K, BLOCK, BLOCK), jnp.float32) ** level_of(key_of[0], (NBX, NBY, K, BLOCK, BLOCK), ((0, 16), (1, 8)), -0.2, 0.2)), 0.019897461, 1.0).astype(jnp.bfloat16),
        "columns": draw_columns(jax.random.fold_in(key_of[3], 71), 0),
        "panel": draw_panel(jax.random.fold_in(key_of[3], 71), 0),
    }


def apply_rows(values, columns, scaled):
    table = scaled.reshape(NBX * NBY, BLOCK, PANEL)

    def one_row(args):
        vrow, crow = args
        picked = table[crow].astype(jnp.float32)
        return jnp.einsum('nkij,nkjc->nic', vrow.astype(jnp.float32), picked, precision=lax.Precision.HIGHEST)
    return lax.map(one_row, (values, columns))

def gram_pair(left, right):
    flat_left = left.reshape(-1, PANEL)
    flat_right = right.reshape(-1, PANEL)
    return jnp.dot(flat_left.T, flat_right, precision=lax.Precision.HIGHEST) / ROWS

def lower_inverse(gram):
    factor = jnp.linalg.cholesky(gram)
    ident = jnp.eye(PANEL, dtype=gram.dtype)
    return lax.linalg.triangular_solve(factor, ident, left_side=True, lower=True)

def reference(values, columns, panel):
    degree = lax.map(lambda vrow: lax.optimization_barrier(jnp.sum(vrow.astype(jnp.float32), axis=(1, 3))), values)
    scale = 1.0 / jnp.sqrt(degree)
    current = panel
    iterate = panel
    inverse = None
    first = None
    for step in range(2):
        scaled = (scale[..., None] * current).astype(jnp.bfloat16)
        iterate = scale[..., None] * apply_rows(values, columns, scaled)
        inverse = lower_inverse(gram_pair(iterate, iterate))
        current = jnp.dot(iterate.reshape(-1, PANEL), inverse.T, precision=lax.Precision.HIGHEST).reshape(iterate.shape)
        if step == 0:
            first = current
    scaled = (scale[..., None] * iterate).astype(jnp.bfloat16)
    image = scale[..., None] * apply_rows(values, columns, scaled)
    moment = gram_pair(iterate, image)
    ritz = jnp.dot(jnp.dot(inverse, moment, precision=lax.Precision.HIGHEST), inverse.T, precision=lax.Precision.HIGHEST)
    return (first, current, ritz)
```

```python
import functools

import jax
import jax.numpy as jnp
from jax import lax
from jax.experimental import pallas as pl
from jax.experimental.pallas import tpu as pltpu
from jax.sharding import PartitionSpec as P

NEAR = 8
FAR = 16
STRIP = 16


def near_partner(step):
    gx = lax.axis_index("gx")
    base = (gx // NEAR) * NEAR
    at = lax.rem(gx - base + step, NEAR)
    return at, (base + at, lax.axis_index("gy"))


def far_partner(step):
    gx, gy = lax.axis_index("gx"), lax.axis_index("gy")
    place = (gx // NEAR) * 8 + gy
    to = lax.rem(place + step, FAR)
    return to, ((to // 8) * NEAR + lax.rem(gx, NEAR), lax.rem(to, 8))


def remote(src, dst, send, recv, device):
    return pltpu.make_async_remote_copy(
        src_ref=src, dst_ref=dst, send_sem=send, recv_sem=recv,
        device_id=device, device_id_type=pl.DeviceIdType.MESH,
    )


def strip_of(ref, at):
    return ref.at[pl.ds(pl.multiple_of(at * STRIP, STRIP), STRIP)]


def sum_kernel(mine, out, near_buf, mid, far_buf, done, s1, r1, s2, r2, s3, r3):
    barrier = pltpu.get_barrier_semaphore()
    for step in range(1, NEAR):
        pl.semaphore_signal(barrier, inc=1, device_id=near_partner(step)[1], device_id_type=pl.DeviceIdType.MESH)
    for step in range(1, FAR):
        pl.semaphore_signal(barrier, inc=1, device_id=far_partner(step)[1], device_id_type=pl.DeviceIdType.MESH)
    pl.semaphore_wait(barrier, NEAR + FAR - 2)
    gx, gy = lax.axis_index("gx"), lax.axis_index("gy")
    near = lax.rem(gx, NEAR)
    far = (gx // NEAR) * 8 + gy

    first = []
    for step in range(1, NEAR):
        at, device = near_partner(step)
        copy = remote(strip_of(mine, at), near_buf.at[near], s1.at[step], r1.at[step], device)
        copy.start()
        first.append(copy)
    near_buf[near] = strip_of(mine, near)[...]
    for copy in first:
        copy.wait()
    part = near_buf[0]
    for i in range(1, NEAR):
        part = part + near_buf[i]
    mid[...] = part
    far_buf[far] = part
    second = []
    for step in range(1, FAR):
        _, device = far_partner(step)
        copy = remote(mid, far_buf.at[far], s2.at[step], r2.at[step], device)
        copy.start()
        second.append(copy)
    for copy in second:
        copy.wait()
    part = far_buf[0]
    for i in range(1, FAR):
        part = part + far_buf[i]
    done[...] = part
    strip_of(out, near)[...] = part
    third = []
    for step in range(1, NEAR):
        _, device = near_partner(step)
        copy = remote(done, strip_of(out, near), s3.at[step], r3.at[step], device)
        copy.start()
        third.append(copy)
    for copy in third:
        copy.wait()


def sum_all(mine, ident):
    dma = pltpu.SemaphoreType.DMA
    return pl.pallas_call(
        sum_kernel,
        out_shape=jax.ShapeDtypeStruct(mine.shape, jnp.float32),
        in_specs=[pl.BlockSpec(memory_space=pltpu.VMEM)],
        out_specs=pl.BlockSpec(memory_space=pltpu.VMEM),
        scratch_shapes=[
            pltpu.VMEM((NEAR, STRIP, 128), jnp.float32),
            pltpu.VMEM((STRIP, 128), jnp.float32),
            pltpu.VMEM((FAR, STRIP, 128), jnp.float32),
            pltpu.VMEM((STRIP, 128), jnp.float32),
            dma((NEAR,)), dma((NEAR,)), dma((FAR,)), dma((FAR,)), dma((NEAR,)), dma((NEAR,)),
        ],
        compiler_params=pltpu.CompilerParams(collective_id=ident, has_side_effects=True),
        name="sum_all_%d" % ident,
    )(mine)
def padded_2(cells, sides, width):
    for axis, dim in sides:
        count = lax.axis_size(axis)
        ends = count - 1
        head = lax.slice_in_dim(cells, 0, width, axis=dim)
        tail = lax.slice_in_dim(cells, cells.shape[dim] - width, cells.shape[dim], axis=dim)
        cells = jnp.concatenate(
            [
                lax.ppermute(tail, axis, [(i, (i + 1) % count) for i in range(ends)]),
                cells,
                lax.ppermute(head, axis, [((i + 1) % count, i) for i in range(ends)]),
            ],
            axis=dim,
        )
    return cells


def lower_inverse(gram):
    factor = jnp.linalg.cholesky(gram)
    width = gram.shape[0]
    ident = jnp.eye(width, dtype=jnp.float32)
    return lax.linalg.triangular_solve(factor, ident, left_side=True, lower=True)


def on_device(values, columns, panel):
    bx_dev, by_dev, blk, width = panel.shape
    nby_all = by_dev * lax.axis_size("gy")
    rows_all = bx_dev * by_dev * blk * lax.axis_size("gx") * lax.axis_size("gy")
    degree = jnp.sum(values, axis=(2, 4), dtype=jnp.float32)
    scale = 1.0 / jnp.sqrt(degree)
    local_x = columns // nby_all - lax.axis_index("gx") * bx_dev + 1
    local_y = columns % nby_all - lax.axis_index("gy") * by_dev + 1
    flat_index = local_x * (by_dev + 2) + local_y

    def apply_rows(scaled):
        padded = padded_2(scaled, (("gx", 0), ("gy", 1)), 1)
        table = padded.reshape(-1, blk, width)
        picked = table[flat_index]
        product = jnp.einsum(
            "abkij,abkjc->abic", values, picked, preferred_element_type=jnp.float32
        )
        return scale[..., None] * product

    def local_pair(left, right):
        return jnp.dot(
            left.reshape(-1, width).T, right.reshape(-1, width), precision=lax.Precision.HIGHEST
        )

    def normalize(iterate, inverse):
        flat = jnp.dot(iterate.reshape(-1, width), inverse.T, precision=lax.Precision.HIGHEST)
        return flat.reshape(iterate.shape)

    scaled = (scale[..., None] * panel).astype(jnp.bfloat16)
    first_iterate = apply_rows(scaled)
    first_gram = sum_all(local_pair(first_iterate, first_iterate), 0) / rows_all
    first_inverse = lower_inverse(first_gram)
    current = normalize(first_iterate, first_inverse)
    scaled = (scale[..., None] * current).astype(jnp.bfloat16)
    iterate = apply_rows(scaled)
    gram_sum = sum_all(local_pair(iterate, iterate), 1)
    inverse = lower_inverse(gram_sum / rows_all)
    image = apply_rows((scale[..., None] * iterate).astype(jnp.bfloat16))
    moment = sum_all(local_pair(iterate, image), 2) / rows_all
    embedding = normalize(iterate, inverse)
    ritz = jnp.dot(
        jnp.dot(inverse, moment, precision=lax.Precision.HIGHEST),
        inverse.T,
        precision=lax.Precision.HIGHEST,
    )
    return (current, embedding, ritz)


def solution(mesh):
    in_specs = (P("gx", "gy", None, None, None), P("gx", "gy", None), P("gx", "gy", None, None))
    out_specs = (P("gx", "gy", None, None), P("gx", "gy", None, None), P())
    return jax.shard_map(
        on_device, mesh=mesh, in_specs=in_specs, out_specs=out_specs, check_vma=False
    )
```

```python
import functools

import jax
import jax.numpy as jnp
from jax import lax
from jax.experimental import pallas as pl
from jax.experimental.pallas import tpu as pltpu
from jax.sharding import PartitionSpec as P

NEAR = 8
FAR = 16
STRIP = 16
BX, BY, K, N = 8, 4, 6, 128
MESH = pl.DeviceIdType.MESH
F32, BF16 = jnp.float32, jnp.bfloat16
UP, DOWN, CORNER = 16, 17, 18
COPIES = 22


def where_am_i():
    gx, gy = lax.axis_index("gx"), lax.axis_index("gy")
    return gx, gy, lax.rem(gx, NEAR), (gx // NEAR) * 8 + gy


def near_partner(step):
    gx, gy, near, _ = where_am_i()
    at = lax.rem(near + step, NEAR)
    return at, (gx - near + at, gy)


def far_partner(step):
    _, _, near, far = where_am_i()
    to = lax.rem(far + step, FAR)
    return ((to // 8) * NEAR + near, lax.rem(to, 8))


def beside(dx, dy):
    gx, gy, _, _ = where_am_i()
    return (lax.rem(gx + dx + 16, 16), lax.rem(gy + dy + 8, 8))


def remote(src, dst, send, recv, device):
    return pltpu.make_async_remote_copy(
        src_ref=src, dst_ref=dst, send_sem=send, recv_sem=recv, device_id=device, device_id_type=MESH
    )


def greet():
    barrier = pltpu.get_barrier_semaphore()
    partners = [near_partner(s)[1] for s in range(1, NEAR)] + [far_partner(s) for s in range(1, FAR)]
    partners += [beside(dx, dy) for dx in (-1, 0, 1) for dy in (-1, 0, 1) if dx or dy]
    for device in partners:
        pl.semaphore_signal(barrier, inc=1, device_id=device, device_id_type=MESH)
    return functools.partial(pl.semaphore_wait, barrier, len(partners))


def strip_of(ref, at):
    return ref.at[pl.ds(pl.multiple_of(at * STRIP, STRIP), STRIP)]


class Sum:
    def __init__(self, mine, near_buf, mid, far_buf, done, out, near_sems, far_sems):
        self.mine, self.near_buf, self.mid, self.far_buf = mine, near_buf, mid, far_buf
        self.done, self.out = done, out
        _, _, self.near, self.far = where_am_i()
        self.first, self.second, self.third = [], [], []
        for s in range(1, NEAR):
            at, device = near_partner(s)
            self.first.append(remote(
                strip_of(mine, at), near_buf.at[self.near], near_sems.at[0, s], near_sems.at[1, s], device))
            self.third.append(remote(
                done, strip_of(out, self.near), near_sems.at[2, s], near_sems.at[3, s], device))
        for s in range(1, FAR):
            self.second.append(remote(
                mid, far_buf.at[self.far], far_sems.at[0, s], far_sems.at[1, s], far_partner(s)))

    def begin(self):
        for copy in self.first:
            copy.start()
        self.near_buf[self.near] = strip_of(self.mine, self.near)[...]

    def middle(self):
        for copy in self.first:
            copy.wait_recv()
        part = self.near_buf[0]
        for i in range(1, NEAR):
            part = part + self.near_buf[i]
        self.mid[...] = part
        self.far_buf[self.far] = part
        for copy in self.second:
            copy.start()

    def last(self):
        for copy in self.second:
            copy.wait_recv()
        part = self.far_buf[0]
        for i in range(1, FAR):
            part = part + self.far_buf[i]
        self.done[...] = part
        strip_of(self.out, self.near)[...] = part
        for copy in self.third:
            copy.start()

    def end(self):
        for copy in self.third:
            copy.wait_recv()

    def drain(self):
        for copy in self.first + self.second + self.third:
            copy.wait_send()


class Rim:
    def __init__(self, own, table, send, recv):
        self.own, self.table, self.send, self.recv = own, table, send, recv

    def put(self, p, q, block):
        self.own[p, q] = block
        self.table[p + 1, q + 1] = block

    def copy(self, at, src, dst, device):
        return remote(src, dst, self.send.at[at], self.recv.at[at], device)

    def left(self, p):
        return self.copy(p, self.own.at[p, 0], self.table.at[p + 1, 5], beside(0, -1))

    def right(self, p):
        return self.copy(p + 8, self.own.at[p, 3], self.table.at[p + 1, 0], beside(0, 1))

    def sides(self, p):
        return [self.left(p), self.right(p)]

    def ends(self):
        own, t = self.own, self.table
        inner = pl.ds(1, 4)
        return [
            self.copy(UP, own.at[0], t.at[9, inner], beside(-1, 0)),
            self.copy(DOWN, own.at[7], t.at[0, inner], beside(1, 0)),
            self.copy(CORNER, own.at[0, 0], t.at[9, 5], beside(-1, -1)),
            self.copy(CORNER + 1, own.at[0, 3], t.at[9, 0], beside(-1, 1)),
            self.copy(CORNER + 2, own.at[7, 0], t.at[0, 5], beside(1, -1)),
            self.copy(CORNER + 3, own.at[7, 3], t.at[0, 0], beside(1, 1)),
        ]

    def drain(self):
        @pl.loop(0, BX)
        def _(p):
            for copy in self.sides(p):
                copy.wait_send()

        for copy in self.ends():
            copy.wait_send()


def pieces(x):
    high = x.astype(BF16)
    rest = x - high.astype(F32)
    mid = rest.astype(BF16)
    low = (rest - mid.astype(F32)).astype(BF16)
    return high, mid, low


def contract_rows(a, b):
    return lax.dot_general(a, b, (((0,), (0,)), ((), ())), preferred_element_type=F32)


def pair(left, right, wide, thin_a, thin_b):
    for total in (wide, thin_a, thin_b):
        total[...] = jnp.zeros(total.shape, F32)

    @pl.loop(0, 8)
    def _(c):
        lh, lm, ll = pieces(left[pl.ds(c * 4, 4)].reshape(512, N))
        if right is None:
            rh, rm, rl = lh, lm, ll
        else:
            rh, rm, rl = pieces(right[pl.ds(c * 4, 4)].reshape(512, N))
        big = contract_rows(jnp.concatenate([lh, lm], 1), jnp.concatenate([rh, rm], 1))
        small = contract_rows(lh, rl)
        other = None if right is None else contract_rows(ll, rh)
        wide[...] += big
        thin_a[...] += small
        if other is not None:
            thin_b[...] += other

    small = thin_a[...]
    small = small + (small.T if right is None else thin_b[...])
    return wide[:N, :N] + (wide[:N, N:] + wide[N:, :N] + (wide[N:, N:] + small))


def factor_block(b, work, inverse):
    at = 8 * b
    lane = lax.broadcasted_iota(jnp.int32, (8, N), 1)
    rows = [work[pl.ds(at + c, 8, stride=0), :] for c in range(8)]
    a = [[jnp.broadcast_to(rows[i][:, at + k : at + k + 1], (8, N)) for k in range(i + 1)] for i in range(8)]
    rows = [jnp.where((lane >= at) & (lane < at + 8), jnp.where(lane == at + c, 1.0, 0.0), rows[c]) for c in range(8)]
    out = []
    for t in range(8):
        r = lax.rsqrt(a[t][t])
        r = r * (1.5 - (0.5 * a[t][t]) * (r * r))
        new = rows[t] * r
        out.append(new)
        for i in range(t + 1, 8):
            a[i][t] = a[i][t] * r
        for i in range(t + 1, 8):
            for k in range(t + 1, i + 1):
                a[i][k] = a[i][k] - a[i][t] * a[k][t]
            rows[i] = rows[i] - a[i][t] * new
    sub = lax.broadcasted_iota(jnp.int32, (8, N), 0)
    block = out[0]
    for i in range(1, 8):
        block = jnp.where(sub == i, out[i], block)
    inverse[pl.ds(at, 8), :] = jnp.where(lane <= at + sub, block, 0.0)
    if b < 15:
        h, m, l = (x.astype(F32) for x in pieces(block))
        left = [jnp.where(lane >= at + 8, x, 0.0) for x in (h, m, l)]
        hl, ml, ll = left
        lefts = jnp.concatenate([hl, ml, hl, ml, hl, ll], 0).astype(BF16)
        rights = jnp.concatenate([h, h, m, m, l, h], 0).astype(BF16)
        update = contract_rows(lefts, rights)
        below = pl.ds(at + 8, N - at - 8)
        full = lax.broadcasted_iota(jnp.int32, (N - at - 8, N), 1)
        old = work[below, :]
        work[below, :] = jnp.where((full >= at) & (full < at + 8), 0.0, old) - update[at + 8 :]


def times_transposed(x, parts):
    h, m, l = pieces(x)
    bh, bm, bl = parts
    dot = functools.partial(jnp.dot, preferred_element_type=F32)
    deep = jnp.concatenate([h, m], 1)
    big = dot(deep, jnp.concatenate([jnp.concatenate([bh, bh], 0), jnp.concatenate([bm, bm], 0)], 1))
    small = dot(jnp.concatenate([h, l], 1), jnp.concatenate([bl, bh], 0))
    return big[:, :N] + (big[:, N:] + small)


def main_kernel(
    cols, values_hbm, panel_hbm, first_hbm, iterate_hbm, inverse_out, moment_out,
    values, panel, scale, owns, tables, y1, y2, q1, wide, thin_a, thin_b, work, inv1,
    sums_mine, sums_near, sums_mid, sums_far, sums_done, sums_out,
    load_sems, near_sems, far_sems, rim_send, rim_recv,
):
    gx, gy, _, _ = where_am_i()
    rims = [Rim(owns[i], tables[i], rim_send.at[i], rim_recv.at[i]) for i in range(3)]
    sums = [
        Sum(sums_mine.at[i], sums_near.at[i], sums_mid.at[i], sums_far.at[i], sums_done.at[i],
            moment_out if i == 2 else sums_out.at[i], near_sems.at[i], far_sems.at[i])
        for i in range(3)
    ]

    def load(p):
        four = pl.ds(p * 4, 4)
        return [
            pltpu.make_async_copy(values_hbm.at[p], values.at[four], load_sems.at[p]),
            pltpu.make_async_copy(panel_hbm.at[p], panel.at[four], load_sems.at[p + 8]),
        ]

    for p in range(BX):
        for copy in load(p):
            copy.start()
    met = greet()
    met()

    ones = jnp.ones((2 * N, N), BF16)

    @pl.loop(0, BX)
    def _(p):
        for copy in load(p):
            copy.wait()
        for q in range(BY):
            i = p * BY + q
            degree = jnp.zeros((N, N), F32)
            for j in range(3):
                both = jnp.concatenate([values[i, 2 * j], values[i, 2 * j + 1]], 1)
                degree = degree + jnp.dot(both, ones, preferred_element_type=F32)
            s = 1.0 / jnp.sqrt(degree)
            scale[i] = s
            rims[0].put(p, q, (s * panel[i]).astype(BF16))
        for copy in rims[0].sides(p):
            copy.start()

    for copy in rims[0].ends():
        copy.start()

    def block_row(table, p, q, edge):
        i = p * BY + q
        total = jnp.zeros((N, N), F32)
        for j in range(3):
            picked = []
            for k in (2 * j, 2 * j + 1):
                c = cols[p, q, k]
                at_x = jnp.clip((c >> 5) - gx * BX + edge, 0, BX - 1 + 2 * edge)
                at_y = jnp.clip((c & 31) - gy * BY + edge, 0, BY - 1 + 2 * edge)
                picked.append(table[at_x, at_y])
            both = jnp.concatenate([values[i, 2 * j], values[i, 2 * j + 1]], 1)
            total = total + jnp.dot(both, jnp.concatenate(picked, 0), preferred_element_type=F32)
        return scale[i] * total

    def sweep(rim, put, between=()):
        between = list(between) + [lambda: None] * 2

        @pl.loop(1, BX - 1)
        def _(p):
            for q in (1, 2):
                put(p, q, block_row(rim.own, p, q, 0))

        between[0]()

        @pl.loop(0, BX)
        def _(p):
            for copy in rim.sides(p):
                copy.wait_recv()

        for copy in rim.ends():
            copy.wait_recv()

        @pl.loop(1, BX - 1)
        def _(p):
            for q in (0, 3):
                put(p, q, block_row(rim.table, p, q, 1))

        between[1]()

        @pl.loop(0, 2)
        def _(e):
            for q in range(BY):
                put(e * (BX - 1), q, block_row(rim.table, e * (BX - 1), q, 1))

    def put1(p, q, y):
        y1[p * BY + q] = y

    sweep(rims[0], put1)
    sums_mine[0] = pair(y1, None, wide, thin_a, thin_b)
    sums[0].begin()
    sums[0].middle()
    sums[0].last()
    sums[0].end()
    work[...] = sums_out[0] * (1.0 / 524288.0)
    for b in range(16):
        factor_block(b, work, inv1)
    parts = pieces(inv1[...].T)

    def embed(p, q):
        i = p * BY + q
        out = times_transposed(y1[i], parts)
        q1[i] = out
        rims[1].put(p, q, (scale[i] * out).astype(BF16))

    @pl.loop(0, BX)
    def _(p):
        embed(p, 0)
        embed(p, 3)
        for copy in rims[1].sides(p):
            copy.start()

    @pl.loop(0, 2)
    def _(e):
        embed(e * (BX - 1), 1)
        embed(e * (BX - 1), 2)

    for copy in rims[1].ends():
        copy.start()

    @pl.loop(1, BX - 1)
    def _(p):
        embed(p, 1)
        embed(p, 2)

    first_copy = pltpu.make_async_copy(q1, first_hbm, load_sems.at[16])
    first_copy.start()

    def put2(p, q, y):
        i = p * BY + q
        y2[i] = y
        rims[2].put(p, q, (scale[i] * y).astype(BF16))

    sweep(rims[1], put2)

    @pl.loop(0, BX)
    def _(p):
        for copy in rims[2].sides(p):
            copy.start()

    for copy in rims[2].ends():
        copy.start()
    second_copy = pltpu.make_async_copy(y2, iterate_hbm, load_sems.at[17])
    second_copy.start()
    sums_mine[1] = pair(y2, None, wide, thin_a, thin_b)
    sums[1].begin()
    sweep(rims[2], put1, (sums[1].middle, sums[1].last))
    sums_mine[2] = pair(y2, y1, wide, thin_a, thin_b)
    sums[2].begin()
    sums[1].end()
    work[...] = sums_out[1] * (1.0 / 524288.0)
    for b in range(16):
        if b == 5:
            sums[2].middle()
        if b == 11:
            sums[2].last()
        factor_block(b, work, inverse_out)
    sums[2].end()
    first_copy.wait()
    second_copy.wait()
    for s in sums:
        s.drain()
    for rim in rims:
        rim.drain()


def last_kernel(inverse, moment, iterate, embedding, ritz):
    hi = lax.Precision.HIGHEST
    inv_t = inverse[...].T
    parts = pieces(inv_t)
    embedding[...] = times_transposed(iterate[...], parts)

    @pl.when(pl.program_id(0) == 0)
    def _():
        left = jnp.dot(inverse[...], moment[...] * (1.0 / 524288.0), precision=hi, preferred_element_type=F32)
        ritz[...] = jnp.dot(left, inv_t, precision=hi, preferred_element_type=F32)


def on_device(values, columns, panel):
    dma = pltpu.SemaphoreType.DMA
    vmem = pltpu.VMEM
    any_space = pl.BlockSpec(memory_space=pl.ANY)
    in_vmem = pl.BlockSpec(memory_space=pltpu.VMEM)
    square = jax.ShapeDtypeStruct((N, N), F32)
    tall = jax.ShapeDtypeStruct((BX * BY, N, N), F32)
    blocks = (BX * BY, N, N)
    first, iterate, inverse, moment = pl.pallas_call(
        main_kernel,
        out_shape=(tall, tall, square, square),
        in_specs=[pl.BlockSpec(memory_space=pltpu.SMEM), any_space, any_space],
        out_specs=(any_space, any_space, in_vmem, in_vmem),
        scratch_shapes=[
            vmem((BX * BY, K, N, N), BF16), vmem(blocks, F32), vmem(blocks, F32),
            [vmem((BX, BY, N, N), BF16) for _ in range(3)],
            [vmem((BX + 2, BY + 2, N, N), BF16) for _ in range(3)],
            vmem(blocks, F32), vmem(blocks, F32), vmem(blocks, F32),
            vmem((2 * N, 2 * N), F32), vmem((N, N), F32), vmem((N, N), F32), vmem((N, N), F32), vmem((N, N), F32),
            vmem((3, N, N), F32), vmem((3, NEAR, STRIP, N), F32), vmem((3, STRIP, N), F32),
            vmem((3, FAR, STRIP, N), F32), vmem((3, STRIP, N), F32), vmem((3, N, N), F32),
            dma((18,)), dma((3, 4, NEAR)), dma((3, 2, FAR)), dma((3, COPIES)), dma((3, COPIES)),
        ],
        compiler_params=pltpu.CompilerParams(
            collective_id=0, has_side_effects=True, vmem_limit_bytes=48 * 1024 * 1024),
        name="iterate_all",
    )(columns, values, panel)
    rows = BX * BY * N
    embedding, ritz = pl.pallas_call(
        last_kernel,
        grid=(4,),
        out_shape=(jax.ShapeDtypeStruct((rows, N), F32), square),
        in_specs=[
            pl.BlockSpec((N, N), lambda i: (0, 0)), pl.BlockSpec((N, N), lambda i: (0, 0)),
            pl.BlockSpec((rows // 4, N), lambda i: (i, 0)),
        ],
        out_specs=(pl.BlockSpec((rows // 4, N), lambda i: (i, 0)), pl.BlockSpec((N, N), lambda i: (0, 0))),
        name="embed_last",
    )(inverse, moment, iterate.reshape(rows, N))
    return first.reshape(panel.shape), embedding.reshape(panel.shape), ritz


def solution(mesh):
    in_specs = (P("gx", "gy", None, None, None), P("gx", "gy", None), P("gx", "gy", None, None))
    out_specs = (P("gx", "gy", None, None), P("gx", "gy", None, None), P())
    return jax.shard_map(
        on_device, mesh=mesh, in_specs=in_specs, out_specs=out_specs, check_vma=False
    )
```

```python
import functools

import jax
import jax.numpy as jnp
from jax import lax
from jax.experimental import pallas as pl
from jax.experimental.pallas import tpu as pltpu
from jax.sharding import PartitionSpec as P

NEAR = 8
FAR = 16
STRIP = 16
BX, BY, K, N = 8, 4, 6, 128
MESH = pl.DeviceIdType.MESH
F32, BF16 = jnp.float32, jnp.bfloat16
UP, DOWN, CORNER = 16, 17, 18
COPIES = 22


def where_am_i():
    gx, gy = lax.axis_index("gx"), lax.axis_index("gy")
    return gx, gy, lax.rem(gx, NEAR), (gx // NEAR) * 8 + gy


def near_partner(step):
    gx, gy, near, _ = where_am_i()
    at = lax.rem(near + step, NEAR)
    return at, (gx - near + at, gy)


def far_partner(step):
    _, _, near, far = where_am_i()
    to = lax.rem(far + step, FAR)
    return ((to // 8) * NEAR + near, lax.rem(to, 8))


def beside(dx, dy):
    gx, gy, _, _ = where_am_i()
    return (lax.rem(gx + dx + 16, 16), lax.rem(gy + dy + 8, 8))


def remote(src, dst, send, recv, device):
    return pltpu.make_async_remote_copy(
        src_ref=src, dst_ref=dst, send_sem=send, recv_sem=recv, device_id=device, device_id_type=MESH
    )


def greet():
    barrier = pltpu.get_barrier_semaphore()
    partners = [near_partner(s)[1] for s in range(1, NEAR)] + [far_partner(s) for s in range(1, FAR)]
    partners += [beside(dx, dy) for dx in (-1, 0, 1) for dy in (-1, 0, 1) if dx or dy]
    for device in partners:
        pl.semaphore_signal(barrier, inc=1, device_id=device, device_id_type=MESH)
    return functools.partial(pl.semaphore_wait, barrier, len(partners))


def strip_of(ref, at):
    return ref.at[pl.ds(pl.multiple_of(at * STRIP, STRIP), STRIP)]


class Sum:
    def __init__(self, mine, near_buf, mid, far_buf, done, out, near_sems, far_sems):
        self.mine, self.near_buf, self.mid, self.far_buf = mine, near_buf, mid, far_buf
        self.done, self.out = done, out
        _, _, self.near, self.far = where_am_i()
        self.first, self.second, self.third = [], [], []
        for s in range(1, NEAR):
            at, device = near_partner(s)
            self.first.append(remote(
                strip_of(mine, at), near_buf.at[self.near], near_sems.at[0, s], near_sems.at[1, s], device))
            self.third.append(remote(
                done, strip_of(out, self.near), near_sems.at[2, s], near_sems.at[3, s], device))
        for s in range(1, FAR):
            self.second.append(remote(
                mid, far_buf.at[self.far], far_sems.at[0, s], far_sems.at[1, s], far_partner(s)))

    def begin(self):
        for copy in self.first:
            copy.start()
        self.near_buf[self.near] = strip_of(self.mine, self.near)[...]

    def middle(self):
        for copy in self.first:
            copy.wait_recv()
        part = self.near_buf[0]
        for i in range(1, NEAR):
            part = part + self.near_buf[i]
        self.mid[...] = part
        self.far_buf[self.far] = part
        for copy in self.second:
            copy.start()

    def last(self):
        for copy in self.second:
            copy.wait_recv()
        part = self.far_buf[0]
        for i in range(1, FAR):
            part = part + self.far_buf[i]
        self.done[...] = part
        strip_of(self.out, self.near)[...] = part
        for copy in self.third:
            copy.start()

    def end(self):
        for copy in self.third:
            copy.wait_recv()

    def drain(self):
        for copy in self.first + self.second + self.third:
            copy.wait_send()


class Rim:
    def __init__(self, own, table, send, recv):
        self.own, self.table, self.send, self.recv = own, table, send, recv

    def put(self, p, q, block):
        self.own[p, q] = block
        self.table[p + 1, q + 1] = block

    def copy(self, at, src, dst, device):
        return remote(src, dst, self.send.at[at], self.recv.at[at], device)

    def left(self, p):
        return self.copy(p, self.own.at[p, 0], self.table.at[p + 1, 5], beside(0, -1))

    def right(self, p):
        return self.copy(p + 8, self.own.at[p, 3], self.table.at[p + 1, 0], beside(0, 1))

    def sides(self, p):
        return [self.left(p), self.right(p)]

    def ends(self):
        own, t = self.own, self.table
        inner = pl.ds(1, 4)
        return [
            self.copy(UP, own.at[0], t.at[9, inner], beside(-1, 0)),
            self.copy(DOWN, own.at[7], t.at[0, inner], beside(1, 0)),
            self.copy(CORNER, own.at[0, 0], t.at[9, 5], beside(-1, -1)),
            self.copy(CORNER + 1, own.at[0, 3], t.at[9, 0], beside(-1, 1)),
            self.copy(CORNER + 2, own.at[7, 0], t.at[0, 5], beside(1, -1)),
            self.copy(CORNER + 3, own.at[7, 3], t.at[0, 0], beside(1, 1)),
        ]

    def drain(self):
        @pl.loop(0, BX)
        def _(p):
            for copy in self.sides(p):
                copy.wait_send()

        for copy in self.ends():
            copy.wait_send()


def pieces(x):
    high = x.astype(BF16)
    rest = x - high.astype(F32)
    mid = rest.astype(BF16)
    low = (rest - mid.astype(F32)).astype(BF16)
    return high, mid, low


def contract_rows(a, b):
    return lax.dot_general(a, b, (((0,), (0,)), ((), ())), preferred_element_type=F32)


def pair(left, right, wide, thin_a, thin_b):
    for total in (wide, thin_a, thin_b):
        total[...] = jnp.zeros(total.shape, F32)

    @pl.loop(0, 8)
    def _(c):
        lh, lm, ll = pieces(left[pl.ds(c * 4, 4)].reshape(512, N))
        if right is None:
            rh, rm, rl = lh, lm, ll
        else:
            rh, rm, rl = pieces(right[pl.ds(c * 4, 4)].reshape(512, N))
        big = contract_rows(jnp.concatenate([lh, lm], 1), jnp.concatenate([rh, rm], 1))
        small = contract_rows(lh, rl)
        other = None if right is None else contract_rows(ll, rh)
        wide[...] += big
        thin_a[...] += small
        if other is not None:
            thin_b[...] += other

    small = thin_a[...]
    small = small + (small.T if right is None else thin_b[...])
    return wide[:N, :N] + (wide[:N, N:] + wide[N:, :N] + (wide[N:, N:] + small))


def factor_block(b, work, inverse):
    at = 8 * b
    lane = lax.broadcasted_iota(jnp.int32, (8, N), 1)
    rows = [work[pl.ds(at + c, 8, stride=0), :] for c in range(8)]
    a = [[jnp.broadcast_to(rows[i][:, at + k : at + k + 1], (8, N)) for k in range(i + 1)] for i in range(8)]
    rows = [jnp.where((lane >= at) & (lane < at + 8), jnp.where(lane == at + c, 1.0, 0.0), rows[c]) for c in range(8)]
    out = []
    for t in range(8):
        r = lax.rsqrt(a[t][t])
        r = r * (1.5 - (0.5 * a[t][t]) * (r * r))
        new = rows[t] * r
        out.append(new)
        for i in range(t + 1, 8):
            a[i][t] = a[i][t] * r
        for i in range(t + 1, 8):
            for k in range(t + 1, i + 1):
                a[i][k] = a[i][k] - a[i][t] * a[k][t]
            rows[i] = rows[i] - a[i][t] * new
    sub = lax.broadcasted_iota(jnp.int32, (8, N), 0)
    block = out[0]
    for i in range(1, 8):
        block = jnp.where(sub == i, out[i], block)
    inverse[pl.ds(at, 8), :] = jnp.where(lane <= at + sub, block, 0.0)
    if b < 15:
        h, m, l = (x.astype(F32) for x in pieces(block))
        left = [jnp.where(lane >= at + 8, x, 0.0) for x in (h, m, l)]
        hl, ml, ll = left
        lefts = jnp.concatenate([hl, ml, hl, ml, hl, ll], 0).astype(BF16)
        rights = jnp.concatenate([h, h, m, m, l, h], 0).astype(BF16)
        update = contract_rows(lefts, rights)
        below = pl.ds(at + 8, N - at - 8)
        full = lax.broadcasted_iota(jnp.int32, (N - at - 8, N), 1)
        old = work[below, :]
        work[below, :] = jnp.where((full >= at) & (full < at + 8), 0.0, old) - update[at + 8 :]


def times_transposed(x, parts):
    h, m, l = pieces(x)
    bh, bm, bl = parts
    dot = functools.partial(jnp.dot, preferred_element_type=F32)
    deep = jnp.concatenate([h, m], 1)
    big = dot(deep, jnp.concatenate([jnp.concatenate([bh, bh], 0), jnp.concatenate([bm, bm], 0)], 1))
    small = dot(jnp.concatenate([h, l], 1), jnp.concatenate([bl, bh], 0))
    return big[:, :N] + (big[:, N:] + small)


def main_kernel(
    cols, values_hbm, panel_hbm, q1, y2, inverse_out, moment_out,
    values, panel, scale, owns, tables, scaled, halo, y1, wide, thin_a, thin_b, work, inv1,
    sums_mine, sums_near, sums_mid, sums_far, sums_done, sums_out,
    load_sems, near_sems, far_sems, rim_send, rim_recv,
):
    gx, gy, _, _ = where_am_i()
    rims = {i: Rim(owns[i // 2], tables[i], rim_send.at[i], rim_recv.at[i]) for i in (0, 2)}
    sums = [
        Sum(sums_mine.at[i], sums_near.at[i], sums_mid.at[i], sums_far.at[i], sums_done.at[i],
            moment_out if i == 2 else sums_out.at[i], near_sems.at[i], far_sems.at[i])
        for i in range(3)
    ]

    def load(p):
        four = pl.ds(p * 4, 4)
        return [
            pltpu.make_async_copy(values_hbm.at[p], values.at[four], load_sems.at[p]),
            pltpu.make_async_copy(panel_hbm.at[p], panel.at[four], load_sems.at[p + 8]),
        ]

    for p in range(BX):
        for copy in load(p):
            copy.start()
    met = greet()

    ones = jnp.ones((2 * N, N), BF16)

    @pl.loop(0, BX)
    def _(p):
        for copy in load(p):
            copy.wait()
        for q in range(BY):
            i = p * BY + q
            degree = jnp.zeros((N, N), F32)
            for j in range(3):
                both = jnp.concatenate([values[i, 2 * j], values[i, 2 * j + 1]], 1)
                degree = degree + jnp.dot(both, ones, preferred_element_type=F32)
            s = 1.0 / jnp.sqrt(degree)
            scale[i] = s
            rims[0].put(p, q, (s * panel[i]).astype(BF16))

    met()

    @pl.loop(0, BX)
    def _(p):
        for copy in rims[0].sides(p):
            copy.start()

    for copy in rims[0].ends():
        copy.start()

    def block_row(table, p, q, edge):
        i = p * BY + q
        total = jnp.zeros((N, N), F32)
        for j in range(3):
            picked = []
            for k in (2 * j, 2 * j + 1):
                c = cols[k, q, p]
                at_x = jnp.clip((c >> 5) - gx * BX + edge, 0, BX - 1 + 2 * edge)
                at_y = jnp.clip((c & 31) - gy * BY + edge, 0, BY - 1 + 2 * edge)
                picked.append(table[at_x, at_y])
            both = jnp.concatenate([values[i, 2 * j], values[i, 2 * j + 1]], 1)
            total = total + jnp.dot(both, jnp.concatenate(picked, 0), preferred_element_type=F32)
        return scale[i] * total

    def sweep(rim, put, between=()):
        between = list(between) + [lambda: None] * 2

        @pl.loop(1, BX - 1)
        def _(p):
            for q in (1, 2):
                put(p, q, block_row(rim.own, p, q, 0))

        between[0]()

        @pl.loop(0, BX)
        def _(p):
            for copy in rim.sides(p):
                copy.wait_recv()

        for copy in rim.ends():
            copy.wait_recv()

        @pl.loop(1, BX - 1)
        def _(p):
            for q in (0, 3):
                put(p, q, block_row(rim.table, p, q, 1))

        between[1]()

        @pl.loop(0, 2)
        def _(e):
            for q in range(BY):
                put(e * (BX - 1), q, block_row(rim.table, e * (BX - 1), q, 1))

    def put1(p, q, y):
        i = p * BY + q
        y1[i] = y
        scaled[p, q] = scale[i] * y

    def put3(p, q, y):
        y1[p * BY + q] = y

    sweep(rims[0], put1)
    wide_rim = Rim(scaled, halo, rim_send.at[1], rim_recv.at[1])

    def send_sides(rim, low, high):
        @pl.loop(low, high)
        def _(p):
            for copy in rim.sides(p):
                copy.start()

    def send_ends(rim):
        for copy in rim.ends():
            copy.start()

    def all_here(rim):
        @pl.loop(0, BX)
        def _(p):
            for copy in rim.sides(p):
                copy.wait_recv()

        for copy in rim.ends():
            copy.wait_recv()

    send_sides(wide_rim, 0, 4)
    sums_mine[0] = pair(y1, None, wide, thin_a, thin_b)
    sums[0].begin()
    sums[0].middle()
    sums[0].last()
    send_ends(wide_rim)
    send_sides(wide_rim, 4, BX)
    sums[0].end()
    work[...] = sums_out[0] * (1.0 / 524288.0)
    for b in range(16):
        factor_block(b, work, inv1)
    parts = pieces(inv1[...].T)

    table = tables[1]

    @pl.loop(0, BX)
    def _(p):
        four = pl.ds(p * BY, BY)
        out = times_transposed(y1[four].reshape(BY * N, N), parts).reshape(BY, N, N)
        q1[four] = out
        table[p + 1, pl.ds(1, BY)] = (scale[four] * out).astype(BF16)

    all_here(wide_rim)

    @pl.loop(0, BX)
    def _(p):
        both = jnp.concatenate([halo[p + 1, 0], halo[p + 1, 5]], 0)
        out = times_transposed(both, parts).astype(BF16)
        table[p + 1, 0] = out[:N]
        table[p + 1, 5] = out[N:]

    @pl.loop(0, 2)
    def _(e):
        out = times_transposed(halo[e * (BX + 1)].reshape((BY + 2) * N, N), parts)
        table[e * (BX + 1)] = out.astype(BF16).reshape(BY + 2, N, N)

    def put2(p, q):
        i = p * BY + q
        y = block_row(table, p, q, 1)
        y2[i] = y
        rims[2].put(p, q, (scale[i] * y).astype(BF16))

    @pl.loop(0, BX)
    def _(p):
        put2(p, 0)
        put2(p, 3)
        for copy in rims[2].sides(p):
            copy.start()

    @pl.loop(0, 2)
    def _(e):
        put2(e * (BX - 1), 1)
        put2(e * (BX - 1), 2)

    send_ends(rims[2])

    @pl.loop(1, BX - 1)
    def _(p):
        put2(p, 1)
        put2(p, 2)

    sums_mine[1] = pair(y2, None, wide, thin_a, thin_b)
    sums[1].begin()
    sweep(rims[2], put3, (sums[1].middle, sums[1].last))
    sums_mine[2] = pair(y2, y1, wide, thin_a, thin_b)
    sums[2].begin()
    sums[1].end()
    work[...] = sums_out[1] * (1.0 / 524288.0)
    for b in range(16):
        if b == 11:
            sums[2].middle()
        factor_block(b, work, inverse_out)
    sums[2].last()
    sums[2].end()
    for s in sums:
        s.drain()
    for rim in (rims[0], wide_rim, rims[2]):
        rim.drain()


def last_kernel(inverse, moment, first, iterate, first_out, embedding_out, ritz, embedding, sems):
    first_copy = pltpu.make_async_copy(first, first_out, sems.at[8])
    first_copy.start()
    hi = lax.Precision.HIGHEST
    inv_t = inverse[...].T
    parts = pieces(inv_t)

    def part(c):
        four = pl.ds(c * 4, 4)
        return pltpu.make_async_copy(embedding.at[four], embedding_out.at[four], sems.at[c])

    @pl.loop(0, 8)
    def _(c):
        four = pl.ds(c * 4, 4)
        embedding[four] = times_transposed(iterate[four].reshape(4 * N, N), parts).reshape(4, N, N)
        part(c).start()

    left = jnp.dot(inverse[...], moment[...] * (1.0 / 524288.0), precision=hi, preferred_element_type=F32)
    ritz[...] = jnp.dot(left, inv_t, precision=hi, preferred_element_type=F32)

    @pl.loop(0, 8)
    def _(c):
        part(c).wait()

    first_copy.wait()


def on_device(values, columns, panel):
    dma = pltpu.SemaphoreType.DMA
    vmem = pltpu.VMEM
    any_space = pl.BlockSpec(memory_space=pl.ANY)
    in_vmem = pl.BlockSpec(memory_space=pltpu.VMEM)
    square = jax.ShapeDtypeStruct((N, N), F32)
    tall = jax.ShapeDtypeStruct((BX * BY, N, N), F32)
    blocks = (BX * BY, N, N)
    first, iterate, inverse, moment = pl.pallas_call(
        main_kernel,
        out_shape=(tall, tall, square, square),
        in_specs=[pl.BlockSpec(memory_space=pltpu.SMEM), any_space, any_space],
        out_specs=(in_vmem,) * 4,
        scratch_shapes=[
            vmem((BX * BY, K, N, N), BF16), vmem(blocks, F32), vmem(blocks, F32),
            [vmem((BX, BY, N, N), BF16) for _ in range(2)],
            [vmem((BX + 2, BY + 2, N, N), BF16) for _ in range(3)],
            vmem((BX, BY, N, N), F32), vmem((BX + 2, BY + 2, N, N), F32), vmem(blocks, F32),
            vmem((2 * N, 2 * N), F32), vmem((N, N), F32), vmem((N, N), F32), vmem((N, N), F32), vmem((N, N), F32),
            vmem((3, N, N), F32), vmem((3, NEAR, STRIP, N), F32), vmem((3, STRIP, N), F32),
            vmem((3, FAR, STRIP, N), F32), vmem((3, STRIP, N), F32), vmem((3, N, N), F32),
            dma((16,)), dma((3, 4, NEAR)), dma((3, 2, FAR)), dma((3, COPIES)), dma((3, COPIES)),
        ],
        compiler_params=pltpu.CompilerParams(
            collective_id=0, has_side_effects=True, vmem_limit_bytes=48 * 1024 * 1024),
        name="iterate_all",
    )(columns.transpose(2, 1, 0), values, panel)
    first, embedding, ritz = pl.pallas_call(
        last_kernel,
        out_shape=(tall, tall, square),
        in_specs=[in_vmem] * 4,
        out_specs=(any_space, any_space, in_vmem),
        scratch_shapes=[vmem(blocks, F32), dma((9,))],
        compiler_params=pltpu.CompilerParams(vmem_limit_bytes=16 * 1024 * 1024),
        name="embed_last",
    )(inverse, moment, first, iterate)
    return first.reshape(panel.shape), embedding.reshape(panel.shape), ritz


def solution(mesh):
    in_specs = (P("gx", "gy", None, None, None), P("gx", "gy", None), P("gx", "gy", None, None))
    out_specs = (P("gx", "gy", None, None), P("gx", "gy", None, None), P())
    return jax.shard_map(
        on_device, mesh=mesh, in_specs=in_specs, out_specs=out_specs, check_vma=False
    )
```
